256 devices in a mesh: row: 16 (over x, y_lo, core), col: 16 (over y_hi, z).
Axes of the slice: x: 4, y: 4 (y_hi: 2, y_lo: 2; y = y_hi * 2 + y_lo), z: 8, core: 2. Of those that a mesh axis runs over, the one named last changes fastest.
Arguments:
- x_dosage: bfloat16 [32768, 4096], P('row', 'col'), may hold values from 0 to 2
- y_dosage: bfloat16 [4096, 32768], P('row', 'col'), may hold values from 0 to 2
- freq: float32 [4096], replicated, may hold values from 0.05 to 0.5
- weight: float32 [4096], replicated, may hold values from 0.5 to 3.47
- sex_rows: int32 [32768], P('row'), may hold values 0 or 1
- sex_cols: int32 [32768], P('col'), may hold values 0 or 1
Outputs:
- relation: bfloat16 [32768, 32768], P('row', 'col')
- inbreeding: float32 [32768], P('row')
The draws below stay inside these ranges and needn't reach their ends.
All inputs are finite; a program needn't handle non-finite values. No bound on the sum of `sex_rows` or of `sex_cols` on one device may be relied on, other than what follows from the above.
Results may differ from the reference program's by a relative error of at most 0.0057.
Values may be sent and summed in bfloat16 or wider, within the bound.
A program may use at most 128 MiB of HBM per device.

```python
import math
import jax
import jax.numpy as jnp
from jax import lax

SR = 2048
VG = 256
STEPS = 4
N1 = 32768
N2 = 32768
M = 4096
N_ROW = 16


def freq_of(key):
    return jax.random.uniform(jax.random.fold_in(key, 11), (M,), jnp.float32, 0.05, 0.5)


def draw_freq(key, part):
    return freq_of(key)


def draw_weight(key, part):
    position = jnp.arange(M, dtype=jnp.float32) / jnp.float32(max(M - 1, 1))
    base = jax.random.uniform(jax.random.fold_in(key, 13), (M,), jnp.float32, math.log(0.5), math.log(2.0))
    return jnp.exp(base) * jnp.exp(0.5 * math.log(3.0) * position)


def spread_draw(key, shape):
    unit = jax.random.uniform(jax.random.fold_in(key, 17), shape, jnp.float32, 0.0, 2.0)
    return unit


def draw_x_dosage(key, part):
    freq = freq_of(key)
    unit = spread_draw(jax.random.fold_in(key, 23), (N1, M))
    return (2.0 * freq[None, :] * unit).astype(jnp.bfloat16)


def draw_y_dosage(key, part):
    freq = freq_of(key)
    unit = spread_draw(jax.random.fold_in(key, 29), (M, N2))
    return (2.0 * freq[:, None] * unit).astype(jnp.bfloat16)


def with_ends(entries, rng, least, top_value):
    dims = entries.shape
    index_at = [jax.random.randint(jax.random.fold_in(rng, axis), (), 0, dims[axis]) for axis in range(len(dims))]
    entries = entries.at[tuple(index_at)].set(least)
    longest = dims.index(max(dims))
    index_at[longest] = (index_at[longest] + 1) % dims[longest]
    return entries.at[tuple(index_at)].set(top_value)


def setup_inputs(seed: int = 0) -> dict:
    arg_keys = jax.random.split(jax.random.key(seed), 7)
    x_dosage = draw_x_dosage(jax.random.fold_in(arg_keys[6], 71), 0)
    y_dosage = draw_y_dosage(jax.random.fold_in(arg_keys[6], 71), 0)
    freq = draw_freq(jax.random.fold_in(arg_keys[6], 71), 0)
    weight = draw_weight(jax.random.fold_in(arg_keys[6], 71), 0)
    sex_rows = with_ends((jax.random.randint(arg_keys[4], (N1,), 0, 2) < 1).astype(jnp.int32), jax.random.fold_in(arg_keys[4], 1), 0, 1)
    sex_cols = with_ends((jax.random.randint(arg_keys[5], (N2,), 0, 2) < 1).astype(jnp.int32), jax.random.fold_in(arg_keys[5], 1), 0, 1)
    return dict(x_dosage=x_dosage, y_dosage=y_dosage, freq=freq, weight=weight, sex_rows=sex_rows, sex_cols=sex_cols)


def standardize(dosage, freq, weight, male):
    value = dosage.astype(jnp.float32)
    female_z = weight * (value - 2.0 * freq) / jnp.sqrt(2.0 * freq * (1.0 - freq))
    male_z = weight * (0.5 * value - freq) / jnp.sqrt(freq * (1.0 - freq))
    return jnp.where(male > 0, male_z, female_z).astype(jnp.bfloat16)

def reference(x_dosage, y_dosage, freq, weight, sex_rows, sex_cols):
    zx = standardize(x_dosage, freq[None, :], weight[None, :], sex_rows[:, None])
    zy = standardize(y_dosage, freq[:, None], weight[:, None], sex_cols[None, :])
    scale = jnp.sqrt(jnp.float32(STEPS * VG))
    blocks = []
    for group_row in range(N_ROW):
        total = jnp.zeros((SR, N2), jnp.float32)
        for step in range(STEPS):
            group = (group_row + step) % N_ROW
            left = zx[group_row * SR:(group_row + 1) * SR, group * VG:(group + 1) * VG]
            right = zy[group * VG:(group + 1) * VG, :]
            total = total + jnp.dot(left, right, preferred_element_type=jnp.float32)
        blocks.append((total / scale).astype(jnp.bfloat16))
    relation = jnp.concatenate(blocks, axis=0)
    squares = lax.optimization_barrier(jnp.sum(jnp.square(zx.astype(jnp.float32)), axis=1))
    inbreeding = squares / jnp.float32(M) - 1.0
    return (relation, inbreeding)
```

```python
import functools

import jax
import jax.numpy as jnp
from jax import lax
from jax.experimental import pallas as pl
from jax.experimental.pallas import tpu as pltpu
from jax.sharding import PartitionSpec as P

STEPS = 4
RING = 8
CHUNKS = 16
GROUP = 256
TILE = 256
COMPUTE_ROUND = 15
PER_ROUND = 6
MESH = pl.DeviceIdType.MESH
HALF = 0.7071067811865476


def kernel(
    x_ref, y_ref, freq_arg, weight_arg, sexr_arg, sexc_arg,
    out_ref, inb_ref,
    freq_ref, weight_ref, sexr_ref, sexc_ref, xg, yg, zy, xo, pcol, acol, scol, corr, qz, qs, qp,
    send, recv, esend, ysend, yrecv, qsend, qrecv, lsem,
):
    rows, vg = x_ref.shape
    cols = y_ref.shape[1]
    half = rows // 2
    chunk = half // CHUNKS
    lanes = 128
    n_row, n_col = lax.axis_size("row"), lax.axis_size("col")
    total_vars = freq_ref.shape[0] * lanes
    r, c = lax.axis_index("row"), lax.axis_index("col")
    h, z, core = c // RING, lax.rem(c, RING), lax.rem(r, 2)
    d = lax.rem(z + 2 * RING - lax.rem(r, RING), RING)
    true = (d < STEPS) & (lax.rem(r + d, n_col) == c)
    up = {"row": r, "col": h * RING + lax.rem(z + 1, RING)}
    down = {"row": r, "col": h * RING + lax.rem(z + RING - 1, RING)}
    across = {"row": r, "col": (1 - h) * RING + z}
    mate = {"row": r + 1 - 2 * core, "col": c}
    row_m2 = {"row": lax.rem(r + n_row - 2, n_row), "col": c}
    row_p2 = {"row": lax.rem(r + 2, n_row), "col": c}
    row_m3 = {"row": lax.rem(r + n_row - 3, n_row), "col": c}
    row_3 = {"row": lax.rem(r + n_row - 3 + 6 * core, n_row), "col": c}
    way = (up, down)

    barrier = pltpu.get_barrier_semaphore()
    friends = (up, down, across, mate, row_m2, row_p2, row_3)
    for friend in friends:
        pl.semaphore_signal(barrier, inc=1, device_id=friend, device_id_type=MESH)

    own_cols = pl.ds(pl.multiple_of(lax.rem(d, STEPS) * vg, vg), vg)
    local_xo = pltpu.make_async_copy(x_ref, xo, lsem.at[0])
    local_y = pltpu.make_async_copy(y_ref, yg.at[pl.ds(0, vg)], lsem.at[1])
    local_xg = pltpu.make_async_copy(x_ref, xg.at[:, own_cols], lsem.at[2])
    small = [
        pltpu.make_async_copy(arg, to, lsem.at[3 + at])
        for at, (arg, to) in enumerate(
            ((freq_arg, freq_ref), (weight_arg, weight_ref), (sexr_arg, sexr_ref), (sexc_arg, sexc_ref))
        )
    ]
    local_xo.start()
    local_y.start()
    for copy in small:
        copy.start()

    @pl.when(true)
    def _():
        local_xg.start()

    pl.semaphore_wait(barrier, len(friends))

    def order(side, i):
        if side == 0:
            s = lax.rem(jnp.minimum(d, STEPS - 1) + STEPS - i, STEPS)
            n = lax.rem(d - s + RING, RING)
        else:
            s = lax.rem(jnp.where(d < STEPS, d, 0) + i, STEPS)
            n = lax.rem(s - d + RING, RING)
        return s, n

    def x_copy(side, s, j, from_arg=False, to_across=False):
        at = pl.ds(pl.multiple_of(side * half + j * chunk, chunk), chunk)
        place = xg.at[at, pl.ds(pl.multiple_of(s * vg, vg), vg)]
        return pltpu.make_async_remote_copy(
            src_ref=x_ref.at[at] if from_arg else place,
            dst_ref=place,
            send_sem=esend.at[side, j] if to_across else send.at[side, s, j],
            recv_sem=recv.at[side, s, j],
            device_id=across if to_across else way[side],
            device_id_type=MESH,
        )

    def y_copy(slot_from, slot_to, sem, target, from_arg=False):
        return pltpu.make_async_remote_copy(
            src_ref=y_ref if from_arg else yg.at[pl.ds(slot_from * vg, vg)],
            dst_ref=yg.at[pl.ds(slot_to * vg, vg)],
            send_sem=ysend.at[sem],
            recv_sem=yrecv.at[slot_to],
            device_id=target,
            device_id_type=MESH,
        )

    y_mate = y_copy(0, 1, 0, mate, True)
    y_two = y_copy(0, 2, 1, row_m2, True)
    y_three = y_copy(0, 3, 2, row_m3, True)
    y_relay1 = y_copy(2, 1, 3, mate)
    y_relay3 = y_copy(2, 3, 3, mate)

    def spread(vector):
        return jnp.broadcast_to(vector, (lanes, lanes)).T

    def tables():
        for copy in small:
            copy.wait()
        for s in range(STEPS):
            for part in range(vg // lanes):
                at = lax.rem(r + s, n_row) * (vg // lanes) + part
                f, w = freq_ref[pl.ds(at, 1), :], weight_ref[pl.ds(at, 1), :]
                to = pl.ds(s * vg + part * lanes, lanes)
                pcol[to, :] = spread(2.0 * f)
                acol[to, :] = spread(w * w / (2.0 * f * (1.0 - f)) / jnp.sqrt(jnp.float32(STEPS * vg)))
        for g in range(rows // lanes):
            scale = jnp.where(sexr_ref[pl.ds(g, 1), :] > 0, HALF, 1.0).astype(jnp.float32)
            scol[pl.ds(g * lanes, lanes), :] = spread(scale)

    def squares():
        local_xo.wait()
        parts = vg // lanes
        ps, scales = [], []
        for part in range(parts):
            at = c * parts + part
            f, w = freq_ref[pl.ds(at, 1), :], weight_ref[pl.ds(at, 1), :]
            ps.append(2.0 * f)
            scales.append(w / jnp.sqrt(2.0 * f * (1.0 - f)))

        @pl.loop(0, rows // lanes)
        def _(g):
            block = xo[pl.ds(pl.multiple_of(g * lanes, lanes), lanes), :].astype(jnp.float32)
            summed = jnp.zeros((lanes, lanes), jnp.float32)
            for part in range(parts):
                value = (block[:, part * lanes:(part + 1) * lanes] - ps[part]) * scales[part]
                summed = summed + value * value
            line = jnp.sum(summed.T, axis=0, keepdims=True)
            line = jnp.where(sexr_ref[pl.ds(g, 1), :] > 0, 0.5 * line, line)
            qz[z, pl.ds(g, 1), :] = line

    def q_copy(side, step):
        shift = step if side else RING - step
        at = lax.rem(z + shift, RING)
        return pltpu.make_async_remote_copy(
            src_ref=qz.at[at], dst_ref=qz.at[at],
            send_sem=qsend.at[side, step], recv_sem=qrecv.at[side, step],
            device_id=way[side], device_id_type=MESH,
        )

    def q_wait(side, step):
        shift = step if side else RING - step
        at = lax.rem(z + shift, RING)
        pltpu.make_async_remote_copy(
            src_ref=qz.at[at], dst_ref=qz.at[at],
            send_sem=qsend.at[side, step], recv_sem=qrecv.at[side, step - 1],
            device_id=way[side], device_id_type=MESH,
        ).wait_recv()

    far = (RING // 2, RING // 2 - 1)

    def q_start():
        for side in range(2):
            q_copy(side, 0).start()

    def q_step(step):
        for side in range(2):
            if step <= far[side]:
                q_wait(side, step)
                if step < far[side]:
                    q_copy(side, step).start()

    q_across = pltpu.make_async_remote_copy(
        src_ref=qs, dst_ref=qp, send_sem=qsend.at[0, 7], recv_sem=qrecv.at[0, 7],
        device_id=across, device_id_type=MESH,
    )

    def q_sum():
        summed = qz[0]
        for at in range(1, RING):
            summed = summed + qz[at]
        qs[...] = summed

    def q_end():
        q_across.wait_recv()
        inb_ref[...] = (qs[...] + qp[...]) / jnp.float32(total_vars) - 1.0

    def transform(slot):
        @pl.loop(0, cols // lanes)
        def _(g):
            at, to = pl.ds(slot * vg, vg), pl.ds(pl.multiple_of(g * lanes, lanes), lanes)
            scale = jnp.where(sexc_ref[pl.ds(g, 1), :] > 0, HALF, 1.0).astype(jnp.float32)
            p = pcol[at, :]
            value = (yg[at, to].astype(jnp.float32) - p) * acol[at, :] * scale
            rounded = value.astype(jnp.bfloat16)
            zy[at, to] = rounded
            sums = jnp.sum(rounded.astype(jnp.float32) * p, axis=0, keepdims=True)
            corr[:, to] = sums if slot == 0 else corr[:, to] + sums

    def piece(side, q, t):
        at = pl.ds(pl.multiple_of(side * half + q * GROUP, GROUP), GROUP)
        to = pl.ds(pl.multiple_of(t * TILE, TILE), TILE)
        total = jnp.dot(xg[at, :], zy[:, to], preferred_element_type=jnp.float32)
        scale = jnp.concatenate([scol[at, :]] * (TILE // lanes), axis=1)
        out_ref[at, to] = ((total - corr[:, to]) * scale).astype(out_ref.dtype)

    def y_first():
        local_y.wait()
        transform(0)

    def y_sends():
        y_two.start()

        @pl.when(core == 0)
        def _():
            y_three.start()

        @pl.when(core == 1)
        def _():
            y_mate.start()

    def y_second():
        y_two.wait_recv()

        @pl.when(core == 0)
        def _():
            y_relay1.start()

        @pl.when(core == 1)
        def _():
            y_relay3.start()

        transform(2)

    def y_near():
        y_mate.wait_recv()
        transform(1)

    def x_own():
        @pl.when(true)
        def _():
            local_xg.wait()

    def y_far():
        y_three.wait_recv()
        transform(3)

    tasks = {
        0: (y_sends, tables), 1: (y_first,), 2: (squares,), 4: (q_start,), 5: (lambda: q_step(1),),
        6: (lambda: q_step(2),), 8: (lambda: q_step(3),), 9: (lambda: q_step(4), q_sum),
        11: (q_across.start,), 12: (y_second,), 13: (y_near,), 14: (y_far, q_end, x_own),
    }

    tiles = cols // TILE
    groups = half // GROUP

    @pl.loop(0, CHUNKS + RING - 1)
    def _(now):
        for side in range(2):
            for i in range(STEPS):
                s, n = order(side, i)
                j = now - n

                @pl.when((j >= 0) & (j < CHUNKS))
                def _():
                    mine = (n == 0) & true

                    @pl.when(mine)
                    def _():
                        x_copy(side, s, j, True).start()
                        x_copy(side, s, j, True, True).start()

                    @pl.when(jnp.logical_not(mine))
                    def _():
                        hop = x_copy(side, s, j)
                        hop.wait_recv()

                        @pl.when(n < RING - 1)
                        def _():
                            hop.start()

        for at, jobs in tasks.items():
            @pl.when(now == at)
            def _():
                for job in jobs:
                    job()

        @pl.when(now >= COMPUTE_ROUND)
        def _():
            @pl.loop(0, PER_ROUND)
            def _(k):
                number = (now - COMPUTE_ROUND) * PER_ROUND + k
                piece(lax.rem(number, 2 * tiles) // tiles, number // (2 * tiles), lax.rem(number, tiles))

    @pl.loop(0, 2 * tiles)
    def _(k):
        piece(k // tiles, groups - 1, lax.rem(k, tiles))

    @pl.loop(0, CHUNKS)
    def _(j):
        for side in range(2):
            for i in range(STEPS):
                s, n = order(side, i)

                @pl.when(n < RING - 1)
                def _():
                    x_copy(side, s, j).wait_send()

            @pl.when(true)
            def _():
                x_copy(side, lax.rem(d, STEPS), j, False, True).wait_send()

    for side in range(2):
        for step in range(far[side]):
            q_copy(side, step).wait_send()
    q_across.wait_send()
    y_two.wait_send()
    y_relay1.wait_send()

    @pl.when(core == 0)
    def _():
        y_three.wait_send()

    @pl.when(core == 1)
    def _():
        y_mate.wait_send()


def local(x_dosage, y_dosage, freq, weight, sex_rows, sex_cols):
    rows, vg = x_dosage.shape
    cols = y_dosage.shape[1]
    lanes = 128
    groups = rows // lanes
    vmem = pl.BlockSpec(memory_space=pltpu.VMEM)
    hbm = pl.BlockSpec(memory_space=pltpu.HBM)
    relation, inbreeding = pl.pallas_call(
        kernel,
        out_shape=(
            pltpu.VMEM((rows, cols), jnp.bfloat16),
            pltpu.VMEM((groups, lanes), jnp.float32),
        ),
        in_specs=[hbm] * 6,
        out_specs=(vmem, vmem),
        scratch_shapes=[
            pltpu.VMEM((freq.shape[0] // lanes, lanes), jnp.float32),
            pltpu.VMEM((freq.shape[0] // lanes, lanes), jnp.float32),
            pltpu.VMEM((groups, lanes), jnp.int32),
            pltpu.VMEM((cols // lanes, lanes), jnp.int32),
            pltpu.VMEM((rows, STEPS * vg), jnp.bfloat16),
            pltpu.VMEM((STEPS * vg, cols), jnp.bfloat16),
            pltpu.VMEM((STEPS * vg, cols), jnp.bfloat16),
            pltpu.VMEM((rows, vg), jnp.bfloat16),
            pltpu.VMEM((STEPS * vg, lanes), jnp.float32),
            pltpu.VMEM((STEPS * vg, lanes), jnp.float32),
            pltpu.VMEM((rows, lanes), jnp.float32),
            pltpu.VMEM((1, cols), jnp.float32),
            pltpu.VMEM((RING, groups, lanes), jnp.float32),
            pltpu.VMEM((groups, lanes), jnp.float32),
            pltpu.VMEM((groups, lanes), jnp.float32),
            pltpu.SemaphoreType.DMA((2, STEPS, CHUNKS)),
            pltpu.SemaphoreType.DMA((2, STEPS, CHUNKS)),
            pltpu.SemaphoreType.DMA((2, CHUNKS)),
            pltpu.SemaphoreType.DMA((4,)),
            pltpu.SemaphoreType.DMA((4,)),
            pltpu.SemaphoreType.DMA((2, 8)),
            pltpu.SemaphoreType.DMA((2, 8)),
            pltpu.SemaphoreType.DMA((7,)),
        ],
        compiler_params=pltpu.CompilerParams(
            collective_id=0, has_side_effects=True, vmem_limit_bytes=48 * 1024 * 1024
        ),
        name="window",
    )(
        x_dosage, y_dosage, freq.reshape(-1, lanes), weight.reshape(-1, lanes),
        sex_rows.reshape(-1, lanes), sex_cols.reshape(-1, lanes),
    )
    return relation, inbreeding.reshape(rows)


def solution(mesh):
    return jax.shard_map(
        local,
        mesh=mesh,
        in_specs=(P("row", "col"), P("row", "col"), P(), P(), P("row"), P("col")),
        out_specs=(P("row", "col"), P("row")),
        check_vma=False,
    )
```

```python
import functools

import jax
import jax.numpy as jnp
from jax import lax
from jax.experimental import pallas as pl
from jax.experimental.pallas import tpu as pltpu
from jax.sharding import PartitionSpec as P

STEPS = 4
RING = 8
CHUNKS = 16
GROUP = 256
TILE = 256
SKEW = 2
COMPUTE_ROUND = 21
PER_ROUND = 6
LATE, SECOND, NEAR, FAR = 10, 17, 19, 20
MESH = pl.DeviceIdType.MESH
HALF = 0.7071067811865476


def kernel(
    x_ref, y_ref, freq_arg, weight_arg, sexr_arg, sexc_arg,
    out_ref, inb_ref,
    freq_ref, weight_ref, sexr_ref, sexc_ref, xg, yg, zy, xo, pcol, acol, scol, corr, qz, qs, qp,
    send, recv, esend, ysend, yrecv, qsend, qrecv, lsem,
):
    rows, vg = x_ref.shape
    cols = y_ref.shape[1]
    half = rows // 2
    chunk = half // CHUNKS
    lanes = 128
    n_row, n_col = lax.axis_size("row"), lax.axis_size("col")
    total_vars = freq_ref.shape[0] * lanes
    r, c = lax.axis_index("row"), lax.axis_index("col")
    h, z, core = c // RING, lax.rem(c, RING), lax.rem(r, 2)
    d = lax.rem(z + 2 * RING - lax.rem(r, RING), RING)
    true = (d < STEPS) & (lax.rem(r + d, n_col) == c)
    up = {"row": r, "col": h * RING + lax.rem(z + 1, RING)}
    down = {"row": r, "col": h * RING + lax.rem(z + RING - 1, RING)}
    across = {"row": r, "col": (1 - h) * RING + z}
    mate = {"row": r + 1 - 2 * core, "col": c}
    row_m2 = {"row": lax.rem(r + n_row - 2, n_row), "col": c}
    row_p2 = {"row": lax.rem(r + 2, n_row), "col": c}
    row_m3 = {"row": lax.rem(r + n_row - 3, n_row), "col": c}
    row_3 = {"row": lax.rem(r + n_row - 3 + 6 * core, n_row), "col": c}
    way = (up, down)

    barrier = pltpu.get_barrier_semaphore()
    friends = (up, down, across, mate, row_m2, row_p2, row_3)
    for friend in friends:
        pl.semaphore_signal(barrier, inc=1, device_id=friend, device_id_type=MESH)

    own_cols = pl.ds(pl.multiple_of(lax.rem(d, STEPS) * vg, vg), vg)
    local_xo = pltpu.make_async_copy(x_ref, xo, lsem.at[0])
    local_y = pltpu.make_async_copy(y_ref, yg.at[pl.ds(0, vg)], lsem.at[1])
    local_xg = pltpu.make_async_copy(x_ref, xg.at[:, own_cols], lsem.at[2])
    small = [
        pltpu.make_async_copy(arg, to, lsem.at[3 + at])
        for at, (arg, to) in enumerate(
            ((freq_arg, freq_ref), (weight_arg, weight_ref), (sexr_arg, sexr_ref), (sexc_arg, sexc_ref))
        )
    ]
    local_xo.start()
    local_y.start()
    for copy in small:
        copy.start()

    @pl.when(true)
    def _():
        local_xg.start()

    pl.semaphore_wait(barrier, len(friends))

    def order(side, i):
        if side == 0:
            s = lax.rem(jnp.minimum(d, STEPS - 1) + STEPS - i, STEPS)
            n = lax.rem(d - s + RING, RING)
        else:
            s = lax.rem(jnp.where(d < STEPS, d, 0) + i, STEPS)
            n = lax.rem(s - d + RING, RING)
        return s, n

    def x_copy(side, s, j, from_arg=False, to_across=False):
        at = pl.ds(pl.multiple_of(side * half + j * chunk, chunk), chunk)
        place = xg.at[at, pl.ds(pl.multiple_of(s * vg, vg), vg)]
        return pltpu.make_async_remote_copy(
            src_ref=x_ref.at[at] if from_arg else place,
            dst_ref=place,
            send_sem=esend.at[side, j] if to_across else send.at[side, s, j],
            recv_sem=recv.at[side, s, j],
            device_id=across if to_across else way[side],
            device_id_type=MESH,
        )

    @pl.when(true)
    def _():
        @pl.loop(0, CHUNKS)
        def _(j):
            for side in range(2):
                x_copy(side, lax.rem(d, STEPS), j, True, True).start()

    def y_copy(slot_from, slot_to, sem, target, from_arg=False):
        return pltpu.make_async_remote_copy(
            src_ref=y_ref if from_arg else yg.at[pl.ds(slot_from * vg, vg)],
            dst_ref=yg.at[pl.ds(slot_to * vg, vg)],
            send_sem=ysend.at[sem],
            recv_sem=yrecv.at[slot_to],
            device_id=target,
            device_id_type=MESH,
        )

    y_mate = y_copy(0, 1, 0, mate, True)
    y_two = y_copy(0, 2, 1, row_m2, True)
    y_three = y_copy(0, 3, 2, row_m3, True)
    y_relay1 = y_copy(2, 1, 3, mate)
    y_relay3 = y_copy(2, 3, 3, mate)

    def spread(vector):
        return jnp.broadcast_to(vector, (lanes, lanes)).T

    def tables():
        for copy in small:
            copy.wait()
        for s in range(STEPS):
            for part in range(vg // lanes):
                at = lax.rem(r + s, n_row) * (vg // lanes) + part
                f, w = freq_ref[pl.ds(at, 1), :], weight_ref[pl.ds(at, 1), :]
                to = pl.ds(s * vg + part * lanes, lanes)
                pcol[to, :] = spread(2.0 * f)
                acol[to, :] = spread(w * w / (2.0 * f * (1.0 - f)) / jnp.sqrt(jnp.float32(STEPS * vg)))
        for g in range(rows // lanes):
            scale = jnp.where(sexr_ref[pl.ds(g, 1), :] > 0, HALF, 1.0).astype(jnp.float32)
            scol[pl.ds(g * lanes, lanes), :] = spread(scale)

    def squares():
        local_xo.wait()
        parts = vg // lanes
        ps, scales = [], []
        for part in range(parts):
            at = c * parts + part
            f, w = freq_ref[pl.ds(at, 1), :], weight_ref[pl.ds(at, 1), :]
            ps.append(2.0 * f)
            scales.append(w / jnp.sqrt(2.0 * f * (1.0 - f)))

        @pl.loop(0, rows // lanes)
        def _(g):
            block = xo[pl.ds(pl.multiple_of(g * lanes, lanes), lanes), :].astype(jnp.float32)
            summed = jnp.zeros((lanes, lanes), jnp.float32)
            for part in range(parts):
                value = (block[:, part * lanes:(part + 1) * lanes] - ps[part]) * scales[part]
                summed = summed + value * value
            line = jnp.sum(summed.T, axis=0, keepdims=True)
            line = jnp.where(sexr_ref[pl.ds(g, 1), :] > 0, 0.5 * line, line)
            qz[z, pl.ds(g, 1), :] = line

    def q_copy(side, step):
        shift = step if side else RING - step
        at = lax.rem(z + shift, RING)
        return pltpu.make_async_remote_copy(
            src_ref=qz.at[at], dst_ref=qz.at[at],
            send_sem=qsend.at[side, step], recv_sem=qrecv.at[side, step],
            device_id=way[side], device_id_type=MESH,
        )

    def q_wait(side, step):
        shift = step if side else RING - step
        at = lax.rem(z + shift, RING)
        pltpu.make_async_remote_copy(
            src_ref=qz.at[at], dst_ref=qz.at[at],
            send_sem=qsend.at[side, step], recv_sem=qrecv.at[side, step - 1],
            device_id=way[side], device_id_type=MESH,
        ).wait_recv()

    far = (RING // 2, RING // 2 - 1)

    def q_start():
        for side in range(2):
            q_copy(side, 0).start()

    def q_step(step):
        for side in range(2):
            if step <= far[side]:
                q_wait(side, step)
                if step < far[side]:
                    q_copy(side, step).start()

    q_across = pltpu.make_async_remote_copy(
        src_ref=qs, dst_ref=qp, send_sem=qsend.at[0, 7], recv_sem=qrecv.at[0, 7],
        device_id=across, device_id_type=MESH,
    )

    def q_sum():
        summed = qz[0]
        for at in range(1, RING):
            summed = summed + qz[at]
        qs[...] = summed

    def q_end():
        q_across.wait_recv()
        inb_ref[...] = (qs[...] + qp[...]) / jnp.float32(total_vars) - 1.0

    def transform(slot):
        @pl.loop(0, cols // lanes)
        def _(g):
            at, to = pl.ds(slot * vg, vg), pl.ds(pl.multiple_of(g * lanes, lanes), lanes)
            scale = jnp.where(sexc_ref[pl.ds(g, 1), :] > 0, HALF, 1.0).astype(jnp.float32)
            p = pcol[at, :]
            value = (yg[at, to].astype(jnp.float32) - p) * acol[at, :] * scale
            rounded = value.astype(jnp.bfloat16)
            zy[at, to] = rounded
            sums = jnp.sum(rounded.astype(jnp.float32) * p, axis=0, keepdims=True)
            corr[:, to] = sums if slot == 0 else corr[:, to] + sums

    def piece(side, q, t):
        at = pl.ds(pl.multiple_of(side * half + q * GROUP, GROUP), GROUP)
        to = pl.ds(pl.multiple_of(t * TILE, TILE), TILE)
        total = jnp.dot(xg[at, :], zy[:, to], preferred_element_type=jnp.float32)
        scale = jnp.concatenate([scol[at, :]] * (TILE // lanes), axis=1)
        out_ref[at, to] = ((total - corr[:, to]) * scale).astype(out_ref.dtype)

    def y_first():
        local_y.wait()
        transform(0)

    y_low = lax.rem(r // 2, 2)

    def y_two_start(low):
        @pl.when(y_low == low)
        def _():
            y_two.start()

    def y_sends():
        y_two_start(1)

        @pl.when(core == 0)
        def _():
            y_three.start()

        @pl.when(core == 1)
        def _():
            y_mate.start()

    def y_second():
        y_two.wait_recv()

        @pl.when(core == 0)
        def _():
            y_relay1.start()

        @pl.when(core == 1)
        def _():
            y_relay3.start()

        transform(2)

    def y_near():
        y_mate.wait_recv()
        transform(1)

    def x_own():
        @pl.when(true)
        def _():
            local_xg.wait()

    def y_far():
        y_three.wait_recv()
        transform(3)

    tasks = {
        0: (y_sends, tables), 1: (y_first,), 2: (squares,), 4: (q_start,), 5: (lambda: q_step(1),),
        6: (lambda: q_step(2),), 8: (lambda: q_step(3),), 9: (lambda: q_step(4), q_sum),
        LATE: (lambda: y_two_start(0),), 11: (q_across.start,), 14: (q_end, x_own), SECOND: (y_second,), NEAR: (y_near,), FAR: (y_far,),
    }

    tiles = cols // TILE
    groups = half // GROUP

    orders = [[order(side, i) for i in range(STEPS)] for side in range(2)]

    @pl.loop(0, CHUNKS + SKEW * (RING - 1))
    def _(now):
        for i in range(STEPS):
            for side in range(2):
                s, n = orders[side][i]
                j = now - SKEW * n

                @pl.when((j >= 0) & (j < CHUNKS))
                def _():
                    mine = (n == 0) & true

                    @pl.when(mine)
                    def _():
                        x_copy(side, s, j, True).start()

                    @pl.when(jnp.logical_not(mine))
                    def _():
                        hop = x_copy(side, s, j)
                        hop.wait_recv()

                        @pl.when(n < RING - 1)
                        def _():
                            hop.start()

        for at, jobs in tasks.items():
            @pl.when(now == at)
            def _():
                for job in jobs:
                    job()

        @pl.when(now >= COMPUTE_ROUND)
        def _():
            @pl.loop(0, PER_ROUND)
            def _(k):
                number = (now - COMPUTE_ROUND) * PER_ROUND + k

                @pl.when(number < 2 * tiles * (groups - 1))
                def _():
                    piece(lax.rem(number, 2 * tiles) // tiles, number // (2 * tiles), lax.rem(number, tiles))

    @pl.loop(0, 2 * tiles)
    def _(k):
        piece(k // tiles, groups - 1, lax.rem(k, tiles))

    @pl.loop(0, CHUNKS)
    def _(j):
        for side in range(2):
            for i in range(STEPS):
                s, n = order(side, i)

                @pl.when(n < RING - 1)
                def _():
                    x_copy(side, s, j).wait_send()

            @pl.when(true)
            def _():
                x_copy(side, lax.rem(d, STEPS), j, False, True).wait_send()

    for side in range(2):
        for step in range(far[side]):
            q_copy(side, step).wait_send()
    q_across.wait_send()
    y_two.wait_send()
    y_relay1.wait_send()

    @pl.when(core == 0)
    def _():
        y_three.wait_send()

    @pl.when(core == 1)
    def _():
        y_mate.wait_send()


def local(x_dosage, y_dosage, freq, weight, sex_rows, sex_cols):
    rows, vg = x_dosage.shape
    cols = y_dosage.shape[1]
    lanes = 128
    groups = rows // lanes
    vmem = pl.BlockSpec(memory_space=pltpu.VMEM)
    hbm = pl.BlockSpec(memory_space=pltpu.HBM)
    relation, inbreeding = pl.pallas_call(
        kernel,
        out_shape=(
            pltpu.VMEM((rows, cols), jnp.bfloat16),
            pltpu.VMEM((groups, lanes), jnp.float32),
        ),
        in_specs=[hbm] * 6,
        out_specs=(vmem, vmem),
        scratch_shapes=[
            pltpu.VMEM((freq.shape[0] // lanes, lanes), jnp.float32),
            pltpu.VMEM((freq.shape[0] // lanes, lanes), jnp.float32),
            pltpu.VMEM((groups, lanes), jnp.int32),
            pltpu.VMEM((cols // lanes, lanes), jnp.int32),
            pltpu.VMEM((rows, STEPS * vg), jnp.bfloat16),
            pltpu.VMEM((STEPS * vg, cols), jnp.bfloat16),
            pltpu.VMEM((STEPS * vg, cols), jnp.bfloat16),
            pltpu.VMEM((rows, vg), jnp.bfloat16),
            pltpu.VMEM((STEPS * vg, lanes), jnp.float32),
            pltpu.VMEM((STEPS * vg, lanes), jnp.float32),
            pltpu.VMEM((rows, lanes), jnp.float32),
            pltpu.VMEM((1, cols), jnp.float32),
            pltpu.VMEM((RING, groups, lanes), jnp.float32),
            pltpu.VMEM((groups, lanes), jnp.float32),
            pltpu.VMEM((groups, lanes), jnp.float32),
            pltpu.SemaphoreType.DMA((2, STEPS, CHUNKS)),
            pltpu.SemaphoreType.DMA((2, STEPS, CHUNKS)),
            pltpu.SemaphoreType.DMA((2, CHUNKS)),
            pltpu.SemaphoreType.DMA((4,)),
            pltpu.SemaphoreType.DMA((4,)),
            pltpu.SemaphoreType.DMA((2, 8)),
            pltpu.SemaphoreType.DMA((2, 8)),
            pltpu.SemaphoreType.DMA((7,)),
        ],
        compiler_params=pltpu.CompilerParams(
            collective_id=0, has_side_effects=True, vmem_limit_bytes=48 * 1024 * 1024
        ),
        name="window",
    )(
        x_dosage, y_dosage, freq.reshape(-1, lanes), weight.reshape(-1, lanes),
        sex_rows.reshape(-1, lanes), sex_cols.reshape(-1, lanes),
    )
    return relation, inbreeding.reshape(rows)


def solution(mesh):
    return jax.shard_map(
        local,
        mesh=mesh,
        in_specs=(P("row", "col"), P("row", "col"), P(), P(), P("row"), P("col")),
        out_specs=(P("row", "col"), P("row")),
        check_vma=False,
    )
```

```python
import functools

import jax
import jax.numpy as jnp
from jax import lax
from jax.experimental import pallas as pl
from jax.experimental.pallas import tpu as pltpu
from jax.sharding import PartitionSpec as P

STEPS = 4
RING = 8
CHUNKS = 16
TILE = 512
SKEW = 2
LATE, SECOND, NEAR, FAR = 12, 19, 21, 21
EDGES, MIDDLES, PER_EDGE, PER_MIDDLE = 22, 26, 2, 2
MESH = pl.DeviceIdType.MESH
HALF = 0.7071067811865476


def kernel(
    x_ref, y_ref, freq_arg, weight_arg, sexr_arg, sexc_arg,
    out_ref, inb_ref,
    freq_ref, weight_ref, sexr_ref, sexc_ref, xg, yg, zy, xo, pcol, acol, scol, corr, qz, qs, qp,
    send, recv, esend, ysend, yrecv, qsend, qrecv, lsem,
):
    rows, vg = x_ref.shape
    cols = y_ref.shape[1]
    half = rows // 2
    chunk = half // CHUNKS
    lanes = 128
    n_row, n_col = lax.axis_size("row"), lax.axis_size("col")
    total_vars = freq_ref.shape[0] * lanes
    r, c = lax.axis_index("row"), lax.axis_index("col")
    h, z, core = c // RING, lax.rem(c, RING), lax.rem(r, 2)
    d = lax.rem(z + 2 * RING - lax.rem(r, RING), RING)
    true = (d < STEPS) & (lax.rem(r + d, n_col) == c)
    up = {"row": r, "col": h * RING + lax.rem(z + 1, RING)}
    down = {"row": r, "col": h * RING + lax.rem(z + RING - 1, RING)}
    across = {"row": r, "col": (1 - h) * RING + z}
    mate = {"row": r + 1 - 2 * core, "col": c}
    row_m2 = {"row": lax.rem(r + n_row - 2, n_row), "col": c}
    row_p2 = {"row": lax.rem(r + 2, n_row), "col": c}
    row_m3 = {"row": lax.rem(r + n_row - 3, n_row), "col": c}
    row_3 = {"row": lax.rem(r + n_row - 3 + 6 * core, n_row), "col": c}
    way = (up, down)

    barrier = pltpu.get_barrier_semaphore()
    friends = (up, down, across, mate, row_m2, row_p2, row_3)
    for friend in friends:
        pl.semaphore_signal(barrier, inc=1, device_id=friend, device_id_type=MESH)

    own_cols = pl.ds(pl.multiple_of(lax.rem(d, STEPS) * vg, vg), vg)
    local_xo = pltpu.make_async_copy(x_ref, xo, lsem.at[0])
    local_y = pltpu.make_async_copy(y_ref, yg.at[pl.ds(0, vg)], lsem.at[1])
    local_xg = pltpu.make_async_copy(x_ref, xg.at[:, own_cols], lsem.at[2])
    small = [
        pltpu.make_async_copy(arg, to, lsem.at[3 + at])
        for at, (arg, to) in enumerate(
            ((freq_arg, freq_ref), (weight_arg, weight_ref), (sexr_arg, sexr_ref), (sexc_arg, sexc_ref))
        )
    ]
    local_xo.start()
    local_y.start()
    for copy in small:
        copy.start()

    @pl.when(true)
    def _():
        local_xg.start()

    pl.semaphore_wait(barrier, len(friends))

    def order(side, i):
        if side == 0:
            s = lax.rem(jnp.minimum(d, STEPS - 1) + STEPS - i, STEPS)
            n = lax.rem(d - s + RING, RING)
        else:
            s = lax.rem(jnp.where(d < STEPS, d, 0) + i, STEPS)
            n = lax.rem(s - d + RING, RING)
        return s, n

    def x_copy(side, s, j, from_arg=False, to_across=False):
        at = pl.ds(pl.multiple_of(j * chunk if side == 0 else rows - (j + 1) * chunk, chunk), chunk)
        place = xg.at[at, pl.ds(pl.multiple_of(s * vg, vg), vg)]
        return pltpu.make_async_remote_copy(
            src_ref=x_ref.at[at] if from_arg else place,
            dst_ref=place,
            send_sem=esend.at[side, j] if to_across else send.at[side, s, j],
            recv_sem=recv.at[side, s, j],
            device_id=across if to_across else way[side],
            device_id_type=MESH,
        )

    @pl.when(true)
    def _():
        @pl.loop(0, CHUNKS)
        def _(j):
            for side in range(2):
                x_copy(side, lax.rem(d, STEPS), j, True, True).start()

    def y_copy(slot_from, slot_to, sem, target, from_arg=False):
        return pltpu.make_async_remote_copy(
            src_ref=y_ref if from_arg else yg.at[pl.ds(slot_from * vg, vg)],
            dst_ref=yg.at[pl.ds(slot_to * vg, vg)],
            send_sem=ysend.at[sem],
            recv_sem=yrecv.at[slot_to],
            device_id=target,
            device_id_type=MESH,
        )

    y_mate = y_copy(0, 1, 0, mate, True)
    y_two = y_copy(0, 2, 1, row_m2, True)
    y_three = y_copy(0, 3, 2, row_m3, True)
    y_relay1 = y_copy(2, 1, 3, mate)
    y_relay3 = y_copy(2, 3, 3, mate)

    def spread(vector):
        return jnp.broadcast_to(vector, (lanes, lanes)).T

    def tables():
        for copy in small:
            copy.wait()
        for s in range(STEPS):
            for part in range(vg // lanes):
                at = lax.rem(r + s, n_row) * (vg // lanes) + part
                f, w = freq_ref[pl.ds(at, 1), :], weight_ref[pl.ds(at, 1), :]
                to = pl.ds(s * vg + part * lanes, lanes)
                pcol[to, :] = spread(2.0 * f)
                acol[to, :] = spread(w * w / (2.0 * f * (1.0 - f)) / jnp.sqrt(jnp.float32(STEPS * vg)))
        for g in range(rows // lanes):
            scale = jnp.where(sexr_ref[pl.ds(g, 1), :] > 0, HALF, 1.0).astype(jnp.float32)
            scol[pl.ds(g * lanes, lanes), :] = spread(scale)

    def squares():
        local_xo.wait()
        parts = vg // lanes
        ps, scales = [], []
        for part in range(parts):
            at = c * parts + part
            f, w = freq_ref[pl.ds(at, 1), :], weight_ref[pl.ds(at, 1), :]
            ps.append(2.0 * f)
            scales.append(w / jnp.sqrt(2.0 * f * (1.0 - f)))

        @pl.loop(0, rows // lanes)
        def _(g):
            block = xo[pl.ds(pl.multiple_of(g * lanes, lanes), lanes), :].astype(jnp.float32)
            summed = jnp.zeros((lanes, lanes), jnp.float32)
            for part in range(parts):
                value = (block[:, part * lanes:(part + 1) * lanes] - ps[part]) * scales[part]
                summed = summed + value * value
            line = jnp.sum(summed.T, axis=0, keepdims=True)
            line = jnp.where(sexr_ref[pl.ds(g, 1), :] > 0, 0.5 * line, line)
            qz[z, pl.ds(g, 1), :] = line

    def q_copy(side, step):
        shift = step if side else RING - step
        at = lax.rem(z + shift, RING)
        return pltpu.make_async_remote_copy(
            src_ref=qz.at[at], dst_ref=qz.at[at],
            send_sem=qsend.at[side, step], recv_sem=qrecv.at[side, step],
            device_id=way[side], device_id_type=MESH,
        )

    def q_wait(side, step):
        shift = step if side else RING - step
        at = lax.rem(z + shift, RING)
        pltpu.make_async_remote_copy(
            src_ref=qz.at[at], dst_ref=qz.at[at],
            send_sem=qsend.at[side, step], recv_sem=qrecv.at[side, step - 1],
            device_id=way[side], device_id_type=MESH,
        ).wait_recv()

    far = (RING // 2, RING // 2 - 1)

    def q_start():
        for side in range(2):
            q_copy(side, 0).start()

    def q_step(step):
        for side in range(2):
            if step <= far[side]:
                q_wait(side, step)
                if step < far[side]:
                    q_copy(side, step).start()

    q_across = pltpu.make_async_remote_copy(
        src_ref=qs, dst_ref=qp, send_sem=qsend.at[0, 7], recv_sem=qrecv.at[0, 7],
        device_id=across, device_id_type=MESH,
    )

    def q_sum():
        summed = qz[0]
        for at in range(1, RING):
            summed = summed + qz[at]
        qs[...] = summed

    def q_end():
        q_across.wait_recv()
        inb_ref[...] = (qs[...] + qp[...]) / jnp.float32(total_vars) - 1.0

    def transform(slot):
        @pl.loop(0, cols // lanes)
        def _(g):
            at, to = pl.ds(slot * vg, vg), pl.ds(pl.multiple_of(g * lanes, lanes), lanes)
            scale = jnp.where(sexc_ref[pl.ds(g, 1), :] > 0, HALF, 1.0).astype(jnp.float32)
            p = pcol[at, :]
            value = (yg[at, to].astype(jnp.float32) - p) * acol[at, :] * scale
            rounded = value.astype(jnp.bfloat16)
            zy[at, to] = rounded
            sums = jnp.sum(rounded.astype(jnp.float32) * p, axis=0, keepdims=True)
            corr[:, to] = sums if slot == 0 else corr[:, to] + sums

    def piece(start, size, t):
        at = pl.ds(pl.multiple_of(start, lanes), size)
        to = pl.ds(pl.multiple_of(t * TILE, TILE), TILE)
        total = jnp.dot(xg[at, :], zy[:, to], preferred_element_type=jnp.float32)
        scale = jnp.concatenate([scol[at, :]] * (TILE // lanes), axis=1)
        out_ref[at, to] = ((total - corr[:, to]) * scale).astype(out_ref.dtype)

    def y_first():
        local_y.wait()
        transform(0)

    def sends_across(row):
        far_d = lax.rem(z + 2 * RING - lax.rem(row, RING), RING)
        return (far_d < STEPS) & (lax.rem(row + far_d, n_col) == c)

    on_path = lax.rem(r - core + n_row - jnp.where(lax.rem(r // 2, 2) == 0, 4, 0), n_row)
    crowded = sends_across(on_path) | sends_across(on_path + 1)

    def y_two_start(held):
        @pl.when(crowded if held else jnp.logical_not(crowded))
        def _():
            y_two.start()

    def y_sends():
        y_two_start(False)

        @pl.when(core == 0)
        def _():
            y_three.start()

        @pl.when(core == 1)
        def _():
            y_mate.start()

    def y_second():
        y_two.wait_recv()

        @pl.when(core == 0)
        def _():
            y_relay1.start()

        @pl.when(core == 1)
        def _():
            y_relay3.start()

        transform(2)

    def y_near():
        y_mate.wait_recv()
        transform(1)

    def x_own():
        @pl.when(true)
        def _():
            local_xg.wait()

    def y_far():
        y_three.wait_recv()
        transform(3)

    tasks = (
        (0, y_sends), (3, tables), (5, y_first), (7, squares), (9, q_start), (11, lambda: q_step(1)),
        (12, lambda: q_step(2)), (13, lambda: q_step(3)), (14, lambda: q_step(4)), (14, q_sum),
        (16, q_across.start), (21, q_end), (21, x_own), (LATE, lambda: y_two_start(True)),
        (SECOND, y_second), (NEAR, y_near), (FAR, y_far),
    )

    tiles = cols // TILE
    edge, middle = rows // 4, rows // 8

    orders = [[order(side, i) for i in range(STEPS)] for side in range(2)]

    @pl.loop(0, CHUNKS + SKEW * (RING - 1))
    def _(now):
        for i in range(STEPS):
            for side in range(2):
                s, n = orders[side][i]
                j = now - SKEW * n

                @pl.when((j >= 0) & (j < CHUNKS))
                def _():
                    mine = (n == 0) & true

                    @pl.when(mine)
                    def _():
                        x_copy(side, s, j, True).start()

                    @pl.when(jnp.logical_not(mine))
                    def _():
                        hop = x_copy(side, s, j)
                        hop.wait_recv()

                        @pl.when(n < RING - 1)
                        def _():
                            hop.start()

        for at, job in tasks:
            pl.when(now == at)(job)

        @pl.when((now >= EDGES) & (now < MIDDLES))
        def _():
            @pl.loop(0, PER_EDGE)
            def _(k):
                number = (now - EDGES) * PER_EDGE + k

                @pl.when(number < 2 * tiles)
                def _():
                    piece(number // tiles * (rows - edge), edge, lax.rem(number, tiles))

        @pl.when(now >= MIDDLES)
        def _():
            @pl.loop(0, PER_MIDDLE)
            def _(k):
                number = (now - MIDDLES) * PER_MIDDLE + k

                @pl.when(number < 2 * tiles)
                def _():
                    piece(edge + number // tiles * (rows - 2 * edge - middle), middle, lax.rem(number, tiles))

    @pl.loop(0, tiles)
    def _(t):
        piece(edge + middle, rows - 2 * (edge + middle), t)

    @pl.loop(0, CHUNKS)
    def _(j):
        for side in range(2):
            for i in range(STEPS):
                s, n = order(side, i)

                @pl.when(n < RING - 1)
                def _():
                    x_copy(side, s, j).wait_send()

            @pl.when(true)
            def _():
                x_copy(side, lax.rem(d, STEPS), j, False, True).wait_send()

    for side in range(2):
        for step in range(far[side]):
            q_copy(side, step).wait_send()
    q_across.wait_send()
    y_two.wait_send()
    y_relay1.wait_send()

    @pl.when(core == 0)
    def _():
        y_three.wait_send()

    @pl.when(core == 1)
    def _():
        y_mate.wait_send()


def local(x_dosage, y_dosage, freq, weight, sex_rows, sex_cols):
    rows, vg = x_dosage.shape
    cols = y_dosage.shape[1]
    lanes = 128
    groups = rows // lanes
    vmem = pl.BlockSpec(memory_space=pltpu.VMEM)
    hbm = pl.BlockSpec(memory_space=pltpu.HBM)
    relation, inbreeding = pl.pallas_call(
        kernel,
        out_shape=(
            pltpu.VMEM((rows, cols), jnp.bfloat16),
            pltpu.VMEM((groups, lanes), jnp.float32),
        ),
        in_specs=[hbm] * 6,
        out_specs=(vmem, vmem),
        scratch_shapes=[
            pltpu.VMEM((freq.shape[0] // lanes, lanes), jnp.float32),
            pltpu.VMEM((freq.shape[0] // lanes, lanes), jnp.float32),
            pltpu.VMEM((groups, lanes), jnp.int32),
            pltpu.VMEM((cols // lanes, lanes), jnp.int32),
            pltpu.VMEM((rows, STEPS * vg), jnp.bfloat16),
            pltpu.VMEM((STEPS * vg, cols), jnp.bfloat16),
            pltpu.VMEM((STEPS * vg, cols), jnp.bfloat16),
            pltpu.VMEM((rows, vg), jnp.bfloat16),
            pltpu.VMEM((STEPS * vg, lanes), jnp.float32),
            pltpu.VMEM((STEPS * vg, lanes), jnp.float32),
            pltpu.VMEM((rows, lanes), jnp.float32),
            pltpu.VMEM((1, cols), jnp.float32),
            pltpu.VMEM((RING, groups, lanes), jnp.float32),
            pltpu.VMEM((groups, lanes), jnp.float32),
            pltpu.VMEM((groups, lanes), jnp.float32),
            pltpu.SemaphoreType.DMA((2, STEPS, CHUNKS)),
            pltpu.SemaphoreType.DMA((2, STEPS, CHUNKS)),
            pltpu.SemaphoreType.DMA((2, CHUNKS)),
            pltpu.SemaphoreType.DMA((4,)),
            pltpu.SemaphoreType.DMA((4,)),
            pltpu.SemaphoreType.DMA((2, 8)),
            pltpu.SemaphoreType.DMA((2, 8)),
            pltpu.SemaphoreType.DMA((7,)),
        ],
        compiler_params=pltpu.CompilerParams(
            collective_id=0, has_side_effects=True, vmem_limit_bytes=48 * 1024 * 1024
        ),
        name="window",
    )(
        x_dosage, y_dosage, freq.reshape(-1, lanes), weight.reshape(-1, lanes),
        sex_rows.reshape(-1, lanes), sex_cols.reshape(-1, lanes),
    )
    return relation, inbreeding.reshape(rows)


def solution(mesh):
    return jax.shard_map(
        local,
        mesh=mesh,
        in_specs=(P("row", "col"), P("row", "col"), P(), P(), P("row"), P("col")),
        out_specs=(P("row", "col"), P("row")),
        check_vma=False,
    )
```

```python
import functools

import jax
import jax.numpy as jnp
from jax import lax
from jax.experimental import pallas as pl
from jax.experimental.pallas import tpu as pltpu
from jax.sharding import PartitionSpec as P

STEPS = 4
RING = 8
CHUNKS = 8
TILE = 512
SKEW = 1
LATE, EARLY, SECOND, LAST = 6, 8, 9, 10
EDGES, MIDDLES = 11, 13
MESH = pl.DeviceIdType.MESH
HALF = 0.7071067811865476


def kernel(
    x_ref, y_ref, freq_arg, weight_arg, sexr_arg, sexc_arg,
    out_ref, inb_ref,
    freq_ref, weight_ref, sexr_ref, sexc_ref, xg, yg, zy, xo, pcol, acol, scol, corr, qz, qs, qp,
    send, recv, esend, ysend, yrecv, qsend, qrecv, lsem,
):
    rows, vg = x_ref.shape
    cols = y_ref.shape[1]
    half = rows // 2
    chunk = half // CHUNKS
    lanes = 128
    n_row, n_col = lax.axis_size("row"), lax.axis_size("col")
    total_vars = freq_ref.shape[0] * lanes
    r, c = lax.axis_index("row"), lax.axis_index("col")
    h, z, core = c // RING, lax.rem(c, RING), lax.rem(r, 2)
    d = lax.rem(z + 2 * RING - lax.rem(r, RING), RING)
    true = (d < STEPS) & (lax.rem(r + d, n_col) == c)
    up = {"row": r, "col": h * RING + lax.rem(z + 1, RING)}
    down = {"row": r, "col": h * RING + lax.rem(z + RING - 1, RING)}
    across = {"row": r, "col": (1 - h) * RING + z}
    mate = {"row": r + 1 - 2 * core, "col": c}
    row_m2 = {"row": lax.rem(r + n_row - 2, n_row), "col": c}
    row_p2 = {"row": lax.rem(r + 2, n_row), "col": c}
    row_m3 = {"row": lax.rem(r + n_row - 3, n_row), "col": c}
    row_3 = {"row": lax.rem(r + n_row - 3 + 6 * core, n_row), "col": c}
    way = (up, down)

    barrier = pltpu.get_barrier_semaphore()
    friends = (up, down, across, mate, row_m2, row_p2, row_3)
    for friend in friends:
        pl.semaphore_signal(barrier, inc=1, device_id=friend, device_id_type=MESH)

    own_cols = pl.ds(pl.multiple_of(lax.rem(d, STEPS) * vg, vg), vg)
    local_xo = pltpu.make_async_copy(x_ref, xo, lsem.at[0])
    local_y = pltpu.make_async_copy(y_ref, yg.at[pl.ds(0, vg)], lsem.at[1])
    local_xg = pltpu.make_async_copy(x_ref, xg.at[:, own_cols], lsem.at[2])
    small = [
        pltpu.make_async_copy(arg, to, lsem.at[3 + at])
        for at, (arg, to) in enumerate(
            ((freq_arg, freq_ref), (weight_arg, weight_ref), (sexr_arg, sexr_ref), (sexc_arg, sexc_ref))
        )
    ]
    local_xo.start()
    local_y.start()
    for copy in small:
        copy.start()

    @pl.when(true)
    def _():
        local_xg.start()

    pl.semaphore_wait(barrier, len(friends))

    def order(side, i):
        if side == 0:
            s = lax.rem(jnp.minimum(d, STEPS - 1) + STEPS - i, STEPS)
            n = lax.rem(d - s + RING, RING)
        else:
            s = lax.rem(jnp.where(d < STEPS, d, 0) + i, STEPS)
            n = lax.rem(s - d + RING, RING)
        return s, n

    def x_copy(side, s, j, from_arg=False, to_across=False):
        at = pl.ds(pl.multiple_of(j * chunk if side == 0 else rows - (j + 1) * chunk, chunk), chunk)
        place = xg.at[at, pl.ds(pl.multiple_of(s * vg, vg), vg)]
        return pltpu.make_async_remote_copy(
            src_ref=x_ref.at[at] if from_arg else place,
            dst_ref=place,
            send_sem=esend.at[side, j] if to_across else send.at[side, s, j],
            recv_sem=recv.at[side, s, j],
            device_id=across if to_across else way[side],
            device_id_type=MESH,
        )

    def exchange():
        @pl.when(true)
        def _():
            @pl.loop(0, CHUNKS)
            def _(j):
                for side in range(2):
                    x_copy(side, lax.rem(d, STEPS), j, True, True).start()

    def y_copy(slot_from, slot_to, sem, target, from_arg=False):
        return pltpu.make_async_remote_copy(
            src_ref=y_ref if from_arg else yg.at[pl.ds(slot_from * vg, vg)],
            dst_ref=yg.at[pl.ds(pl.multiple_of(slot_to * vg, vg), vg)],
            send_sem=ysend.at[sem],
            recv_sem=yrecv.at[slot_to],
            device_id=target,
            device_id_type=MESH,
        )

    y_mate = y_copy(0, 1, 0, mate, True)
    y_two = y_copy(0, 2, 1, row_m2, True)
    y_three = y_copy(0, 3, 2, row_m3, True)
    y_relay1 = y_copy(2, 1, 3, mate)
    y_relay3 = y_copy(2, 3, 3, mate)

    def spread(vector):
        return jnp.broadcast_to(vector, (lanes, lanes)).T

    def tables():
        for copy in small:
            copy.wait()
        for s in range(STEPS):
            for part in range(vg // lanes):
                at = lax.rem(r + s, n_row) * (vg // lanes) + part
                f, w = freq_ref[pl.ds(at, 1), :], weight_ref[pl.ds(at, 1), :]
                to = pl.ds(s * vg + part * lanes, lanes)
                pcol[to, :] = spread(2.0 * f)
                acol[to, :] = spread(w * w / (2.0 * f * (1.0 - f)) / jnp.sqrt(jnp.float32(STEPS * vg)))
        for g in range(rows // lanes):
            scale = jnp.where(sexr_ref[pl.ds(g, 1), :] > 0, HALF, 1.0).astype(jnp.float32)
            scol[pl.ds(g * lanes, lanes), :] = spread(scale)

    def squares():
        local_xo.wait()
        parts = vg // lanes
        ps, scales = [], []
        for part in range(parts):
            at = c * parts + part
            f, w = freq_ref[pl.ds(at, 1), :], weight_ref[pl.ds(at, 1), :]
            ps.append(2.0 * f)
            scales.append(w / jnp.sqrt(2.0 * f * (1.0 - f)))

        @pl.loop(0, rows // lanes)
        def _(g):
            block = xo[pl.ds(pl.multiple_of(g * lanes, lanes), lanes), :].astype(jnp.float32)
            summed = jnp.zeros((lanes, lanes), jnp.float32)
            for part in range(parts):
                value = (block[:, part * lanes:(part + 1) * lanes] - ps[part]) * scales[part]
                summed = summed + value * value
            line = jnp.sum(summed.T, axis=0, keepdims=True)
            line = jnp.where(sexr_ref[pl.ds(g, 1), :] > 0, 0.5 * line, line)
            qz[z, pl.ds(g, 1), :] = line

    def q_copy(side, step):
        shift = step if side else RING - step
        at = lax.rem(z + shift, RING)
        return pltpu.make_async_remote_copy(
            src_ref=qz.at[at], dst_ref=qz.at[at],
            send_sem=qsend.at[side, step], recv_sem=qrecv.at[side, step],
            device_id=way[side], device_id_type=MESH,
        )

    def q_wait(side, step):
        shift = step if side else RING - step
        at = lax.rem(z + shift, RING)
        pltpu.make_async_remote_copy(
            src_ref=qz.at[at], dst_ref=qz.at[at],
            send_sem=qsend.at[side, step], recv_sem=qrecv.at[side, step - 1],
            device_id=way[side], device_id_type=MESH,
        ).wait_recv()

    far = (RING // 2, RING // 2 - 1)

    def q_start():
        for side in range(2):
            q_copy(side, 0).start()

    def q_step(step):
        for side in range(2):
            if step <= far[side]:
                q_wait(side, step)
                if step < far[side]:
                    q_copy(side, step).start()

    q_across = pltpu.make_async_remote_copy(
        src_ref=qs, dst_ref=qp, send_sem=qsend.at[0, 7], recv_sem=qrecv.at[0, 7],
        device_id=across, device_id_type=MESH,
    )

    def q_sum():
        summed = qz[0]
        for at in range(1, RING):
            summed = summed + qz[at]
        qs[...] = summed

    def q_end():
        q_across.wait_recv()
        inb_ref[...] = (qs[...] + qp[...]) / jnp.float32(total_vars) - 1.0

    def transform(slot, first=False):
        @pl.loop(0, cols // lanes)
        def _(g):
            at, to = pl.ds(pl.multiple_of(slot * vg, vg), vg), pl.ds(pl.multiple_of(g * lanes, lanes), lanes)
            scale = jnp.where(sexc_ref[pl.ds(g, 1), :] > 0, HALF, 1.0).astype(jnp.float32)
            p = pcol[at, :]
            value = (yg[at, to].astype(jnp.float32) - p) * acol[at, :] * scale
            rounded = value.astype(jnp.bfloat16)
            zy[at, to] = rounded
            sums = jnp.sum(rounded.astype(jnp.float32) * p, axis=0, keepdims=True)
            corr[:, to] = sums if first else corr[:, to] + sums

    def piece(start, size, t):
        at = pl.ds(pl.multiple_of(start, lanes), size)
        to = pl.ds(pl.multiple_of(t * TILE, TILE), TILE)
        total = jnp.dot(xg[at, :], zy[:, to], preferred_element_type=jnp.float32)
        scale = jnp.concatenate([scol[at, :]] * (TILE // lanes), axis=1)
        out_ref[at, to] = ((total - corr[:, to]) * scale).astype(out_ref.dtype)

    def y_first():
        local_y.wait()
        transform(0, True)

    def sends_across(row):
        far_d = lax.rem(z + 2 * RING - lax.rem(row, RING), RING)
        return (far_d < STEPS) & (lax.rem(row + far_d, n_col) == c)

    on_path = lax.rem(r - core + n_row - jnp.where(lax.rem(r // 2, 2) == 0, 4, 0), n_row)
    crowded = sends_across(on_path) | sends_across(on_path + 1)

    def y_two_start(held):
        @pl.when(crowded if held else jnp.logical_not(crowded))
        def _():
            y_two.start()

    def y_sends():
        y_two_start(False)

        @pl.when(core == 0)
        def _():
            y_three.start()

        @pl.when(core == 1)
        def _():
            y_mate.start()

    def y_second():
        y_two.wait_recv()

        @pl.when(core == 0)
        def _():
            y_relay1.start()

        @pl.when(core == 1)
        def _():
            y_relay3.start()

        transform(2)

    def x_own():
        @pl.when(true)
        def _():
            local_xg.wait()

    def y_early():
        y_copy(0, 1 + 2 * core, 0, mate).wait_recv()
        transform(1 + 2 * core)

    def y_last():
        y_copy(0, 3 - 2 * core, 0, mate).wait_recv()
        transform(3 - 2 * core)

    tasks = (
        (-1, exchange), (-1, y_sends), (1, tables), (2, y_first), (3, squares), (4, q_start), (5, lambda: q_step(1)),
        (6, lambda: q_step(2)), (7, lambda: q_step(3)), (8, lambda: q_step(4)), (8, q_sum),
        (9, q_across.start), (10, x_own), (LATE, lambda: y_two_start(True)),
        (EARLY, y_early), (SECOND, y_second), (LAST, y_last), (12, q_end),
    )

    tiles = cols // TILE
    edge, middle = rows // 4, rows // 8

    orders = [[order(side, i) for i in range(STEPS)] for side in range(2)]

    @pl.loop(0, CHUNKS + SKEW * (RING - 1))
    def _(now):
        for at, job in tasks:
            pl.when(now == at + 1)(job)

        for i in range(STEPS):
            for side in range(2):
                s, n = orders[side][i]
                j = now - SKEW * n

                @pl.when((j >= 0) & (j < CHUNKS))
                def _():
                    mine = (n == 0) & true

                    @pl.when(mine)
                    def _():
                        x_copy(side, s, j, True).start()

                    @pl.when(jnp.logical_not(mine))
                    def _():
                        hop = x_copy(side, s, j)
                        hop.wait_recv()

                        @pl.when(n < RING - 1)
                        def _():
                            hop.start()

            @pl.when((now >= EDGES) & (now < MIDDLES))
            def _():
                number = (now - EDGES) * STEPS + i
                piece(number // tiles * (rows - edge), edge, lax.rem(number, tiles))

            @pl.when(now >= MIDDLES)
            def _():
                number = (now - MIDDLES) * STEPS + i
                piece(edge + number // tiles * (rows - 2 * edge - middle), middle, lax.rem(number, tiles))

    @pl.loop(0, tiles)
    def _(t):
        piece(edge + middle, rows - 2 * (edge + middle), t)

    @pl.loop(0, CHUNKS)
    def _(j):
        for side in range(2):
            for i in range(STEPS):
                s, n = order(side, i)

                @pl.when(n < RING - 1)
                def _():
                    x_copy(side, s, j).wait_send()

            @pl.when(true)
            def _():
                x_copy(side, lax.rem(d, STEPS), j, False, True).wait_send()

    for side in range(2):
        for step in range(far[side]):
            q_copy(side, step).wait_send()
    q_across.wait_send()
    y_two.wait_send()
    y_relay1.wait_send()

    @pl.when(core == 0)
    def _():
        y_three.wait_send()

    @pl.when(core == 1)
    def _():
        y_mate.wait_send()


def local(x_dosage, y_dosage, freq, weight, sex_rows, sex_cols):
    rows, vg = x_dosage.shape
    cols = y_dosage.shape[1]
    lanes = 128
    groups = rows // lanes
    vmem = pl.BlockSpec(memory_space=pltpu.VMEM)
    hbm = pl.BlockSpec(memory_space=pltpu.HBM)
    relation, inbreeding = pl.pallas_call(
        kernel,
        out_shape=(
            pltpu.VMEM((rows, cols), jnp.bfloat16),
            pltpu.VMEM((groups, lanes), jnp.float32),
        ),
        in_specs=[hbm] * 6,
        out_specs=(vmem, vmem),
        scratch_shapes=[
            pltpu.VMEM((freq.shape[0] // lanes, lanes), jnp.float32),
            pltpu.VMEM((freq.shape[0] // lanes, lanes), jnp.float32),
            pltpu.VMEM((groups, lanes), jnp.int32),
            pltpu.VMEM((cols // lanes, lanes), jnp.int32),
            pltpu.VMEM((rows, STEPS * vg), jnp.bfloat16),
            pltpu.VMEM((STEPS * vg, cols), jnp.bfloat16),
            pltpu.VMEM((STEPS * vg, cols), jnp.bfloat16),
            pltpu.VMEM((rows, vg), jnp.bfloat16),
            pltpu.VMEM((STEPS * vg, lanes), jnp.float32),
            pltpu.VMEM((STEPS * vg, lanes), jnp.float32),
            pltpu.VMEM((rows, lanes), jnp.float32),
            pltpu.VMEM((1, cols), jnp.float32),
            pltpu.VMEM((RING, groups, lanes), jnp.float32),
            pltpu.VMEM((groups, lanes), jnp.float32),
            pltpu.VMEM((groups, lanes), jnp.float32),
            pltpu.SemaphoreType.DMA((2, STEPS, CHUNKS)),
            pltpu.SemaphoreType.DMA((2, STEPS, CHUNKS)),
            pltpu.SemaphoreType.DMA((2, CHUNKS)),
            pltpu.SemaphoreType.DMA((4,)),
            pltpu.SemaphoreType.DMA((4,)),
            pltpu.SemaphoreType.DMA((2, 8)),
            pltpu.SemaphoreType.DMA((2, 8)),
            pltpu.SemaphoreType.DMA((7,)),
        ],
        compiler_params=pltpu.CompilerParams(
            collective_id=0, has_side_effects=True, vmem_limit_bytes=48 * 1024 * 1024
        ),
        name="window",
    )(
        x_dosage, y_dosage, freq.reshape(-1, lanes), weight.reshape(-1, lanes),
        sex_rows.reshape(-1, lanes), sex_cols.reshape(-1, lanes),
    )
    return relation, inbreeding.reshape(rows)


def solution(mesh):
    return jax.shard_map(
        local,
        mesh=mesh,
        in_specs=(P("row", "col"), P("row", "col"), P(), P(), P("row"), P("col")),
        out_specs=(P("row", "col"), P("row")),
        check_vma=False,
    )
```
